512 devices in a mesh: ind: 32 (over z, x), snp: 16 (over y, core).
Axes of the slice: x: 4, y: 8, z: 8, core: 2. Of those that a mesh axis runs over, the one named last changes fastest.
Arguments:
- genotype: int32 [16384, 32768], P('ind', 'snp'), may hold values from 0 to 170, as said below
- probe: bfloat16 [24, 32768], P(None, 'snp'), may hold values from -0.03125 to 0.03125
- allele_mean: float32 [32768], P('snp'), may hold values from 0.2 to 1.8
- allele_scale: float32 [32768], P('snp'), may hold values from 0.3 to 3
Outputs:
- projected: float32 [24, 32768], P(None, 'snp')
The draws below stay inside these ranges and needn't reach their ends.
Inputs may be any that keep to these rules, and one draw needn't show every extreme that they name: `genotype`: word r of a column holds the codes of individuals 4 r + k, k = 0 to 3, in bits 2 k and 2 k + 1; every code is 0, 1 or 2.
All inputs are finite; a program needn't handle non-finite values.
Results may differ from the reference program's by a relative error of at most 0.0095.
Values may be sent and summed in bfloat16 or wider, within the bound.
No kernel may reach another device: no remote copies, remote signals or barrier semaphores. Data moves between devices by JAX's collectives and lax.ppermute only.
A program may use at most 64 MiB of HBM per device.

```python
import math
import jax
import jax.numpy as jnp
from jax import lax

RANK = 24
NIND = 65536
NSNP = 32768


def draw_genotype(key, part):
    key_anc, key_cut, key_codes = jax.random.split(key, 3)
    ancestry = jax.random.randint(key_anc, (4, NIND // 4), 0, 4)
    thresholds = jax.random.randint(key_cut, (4, NSNP), 2, 15)
    packed = jnp.zeros((NIND // 4, NSNP), jnp.int32)
    for offset in range(4):
        key_plane = jax.random.fold_in(key_codes, offset)
        key_first, key_second = jax.random.split(key_plane)
        cutoff = thresholds[ancestry[offset]]
        first_draw = jax.random.randint(key_first, (NIND // 4, NSNP), 0, 16)
        second_draw = jax.random.randint(key_second, (NIND // 4, NSNP), 0, 16)
        codes = (first_draw < cutoff).astype(jnp.int32) + (second_draw < cutoff).astype(jnp.int32)
        packed = jnp.bitwise_or(packed, jnp.left_shift(codes, 2 * offset))
    packed = packed.at[0, 0].set(jnp.array(170, jnp.int32))
    packed = packed.at[0, 1].set(jnp.array(0, jnp.int32))
    return packed


def shard_levels(stream_key, shape, cuts, smallest, high):
    def one(position, blocks):
        steps = jax.random.uniform(jax.random.fold_in(jax.random.fold_in(stream_key, 6), position), (blocks,), jnp.float32, smallest / len(cuts), high / len(cuts))
        return jnp.repeat(jnp.exp(steps), shape[position] // blocks).reshape((-1,) + (1,) * (len(shape) - position - 1))

    loudness = one(*cuts[0])
    for cut in cuts[1:]:
        loudness = loudness * one(*cut)
    return loudness


def gaussian(rng, extent, deviation, bound, shards=(), dtype=jnp.bfloat16):
    drawn = jax.random.normal(rng, extent, jnp.float32) * deviation
    if len(shards) > 0:
        drawn = shard_levels(rng, extent, shards, -0.22, 0.18) * drawn
    return jnp.clip(drawn, min=-bound, max=bound).astype(dtype)


def setup_inputs(seed: int = 0) -> dict:
    arg_keys = jax.random.split(jax.random.key(seed), 5)
    return {
        "genotype": draw_genotype(jax.random.fold_in(arg_keys[4], 71), 0),
        "probe": gaussian(arg_keys[1], (RANK, NSNP), NSNP ** -0.5, 0.03125, ((1, 16),)),
        "allele_mean": jnp.clip(0.2 + 1.5999999 * jax.random.uniform(arg_keys[2], (NSNP,), jnp.float32) ** shard_levels(arg_keys[2], (NSNP,), ((0, 16),), -0.2, 0.2), 0.2, 1.8),
        "allele_scale": jnp.clip(jnp.exp(math.log(3.0) - 2.3025851 * jax.random.uniform(arg_keys[3], (NSNP,), jnp.float32) ** shard_levels(arg_keys[3], (NSNP,), ((0, 16),), -0.2, 0.2)), 0.3, 3.0),
    }


def unpack(packed, allele_mean, allele_scale):
    planes = []
    for offset in range(4):
        codes = jnp.bitwise_and(jnp.right_shift(packed, 2 * offset), 3)
        planes.append(((codes.astype(jnp.float32) - allele_mean) * allele_scale).astype(jnp.bfloat16))
    stacked = jnp.stack(planes, axis=1)
    return stacked.reshape(packed.shape[0] * 4, packed.shape[1])

def reference(genotype, probe, allele_mean, allele_scale):
    block_rows = math.gcd(NIND // 4, 32)
    block_count = NIND // 4 // block_rows
    packed_blocks = genotype.reshape(block_count, block_rows, NSNP)

    def sketch_step(carry, packed):
        zed = unpack(packed, allele_mean, allele_scale)
        return (carry, jnp.dot(zed.astype(jnp.float32), probe.T.astype(jnp.float32), preferred_element_type=jnp.float32))
    ignored, pieces = lax.scan(sketch_step, jnp.zeros((), jnp.float32), packed_blocks)
    sketch = pieces.reshape(NIND, RANK).T
    gram = jnp.dot(sketch.astype(jnp.float32), sketch.T.astype(jnp.float32), precision=lax.Precision.HIGHEST, preferred_element_type=jnp.float32)
    lower = jnp.linalg.cholesky(gram)
    basis = jax.scipy.linalg.solve_triangular(lower, sketch, lower=True).astype(jnp.bfloat16)
    basis_blocks = basis.reshape(RANK, block_count, 4 * block_rows).transpose(1, 0, 2)

    def project_step(total, inputs):
        packed, basis_block = inputs
        zed = unpack(packed, allele_mean, allele_scale)
        return (total + jnp.dot(basis_block.astype(jnp.float32), zed.astype(jnp.float32), preferred_element_type=jnp.float32), 0.0)
    projected, ignored_too = lax.scan(project_step, jnp.zeros((RANK, NSNP), jnp.float32), (packed_blocks, basis_blocks))
    return projected
```

```python
import jax
import jax.numpy as jnp
from jax import lax
from jax.experimental import pallas as pl
from jax.experimental.pallas import tpu as pltpu
from jax.sharding import PartitionSpec as P

F32, BF16 = jnp.float32, jnp.bfloat16
NT = (((1,), (1,)), ((), ()))
LANES = 128


def digits(words):
    return jnp.concatenate(
        [jnp.bitwise_and(words, 3 << (2 * p)).astype(F32).astype(BF16) for p in range(4)],
        axis=0,
    )


def sketch_kernel(words_ref, probe_ref, mean_ref, scale_ref, out_ref, weight_ref, shift_ref):
    rank = probe_ref.shape[0]
    step = pl.program_id(0)
    steps = pl.num_programs(0)

    @pl.when(step == 0)
    def _():
        weight = probe_ref[...].astype(F32) * scale_ref[...]
        high = weight.astype(BF16)
        weight_ref[0:rank, :] = high.astype(F32)
        weight_ref[rank : 2 * rank, :] = weight - high.astype(F32)
        shift = jnp.sum(weight * mean_ref[...], axis=1, keepdims=True)
        shift_ref[...] = jnp.broadcast_to(shift, shift_ref.shape)

    rows = words_ref.shape[0]
    both = lax.dot_general(
        digits(words_ref[...]), weight_ref[...].astype(BF16), NT, preferred_element_type=F32
    )
    for p in range(4):
        part = both[p * rows : (p + 1) * rows, :].T
        total = (part[0:rank, :] + part[rank : 2 * rank, :]) * (0.25**p)
        out_ref[p * steps + step] = (total - shift_ref[...]).astype(BF16)


def sketch_partial(genotype, probe, mean, scale):
    words, snps = genotype.shape
    rank = probe.shape[0]
    steps = words // LANES
    whole = lambda g: (0, 0)
    return pl.pallas_call(
        sketch_kernel,
        grid=(steps,),
        in_specs=[
            pl.BlockSpec((LANES, snps), lambda g: (g, 0)),
            pl.BlockSpec((rank, snps), whole),
            pl.BlockSpec((1, snps), whole),
            pl.BlockSpec((1, snps), whole),
        ],
        out_specs=pl.BlockSpec((4 * steps, rank, LANES), lambda g: (0, 0, 0)),
        out_shape=jax.ShapeDtypeStruct((4 * steps, rank, LANES), BF16),
        scratch_shapes=[pltpu.VMEM((2 * rank, snps), F32), pltpu.VMEM((rank, LANES), F32)],
        name="sketch",
    )(genotype, probe, mean, scale)


def gather_kernel(parts_ref, out_ref):
    total = parts_ref[0].astype(F32)
    for source in range(1, parts_ref.shape[0]):
        total = total + parts_ref[source].astype(F32)
    chunk = total.astype(BF16)
    for target in range(out_ref.shape[0]):
        out_ref[target] = chunk


def sum_and_copy(parts):
    return pl.pallas_call(
        gather_kernel, out_shape=jax.ShapeDtypeStruct(parts.shape, BF16), name="sumsnp"
    )(parts)


def project_kernel(words_ref, sketch_ref, mean_ref, scale_ref, out_ref, total_ref):
    chunks, rank, width = sketch_ref.shape
    step = pl.program_id(0)
    steps = pl.num_programs(0)
    left = jnp.concatenate(
        [sketch_ref[p * steps + step].astype(F32) * (0.25**p) for p in range(4)], axis=1
    ).astype(BF16)
    piece = jnp.dot(left, digits(words_ref[...]), preferred_element_type=F32)

    @pl.when(step == 0)
    def _():
        total_ref[...] = piece

    @pl.when(step > 0)
    def _():
        total_ref[...] += piece

    @pl.when(step == steps - 1)
    def _():
        gram = jnp.zeros((rank, rank), F32)
        sums = jnp.zeros((rank, width), F32)
        for b in range(chunks):
            block = sketch_ref[b]
            gram = gram + lax.dot_general(block, block, NT, preferred_element_type=F32)
            sums = sums + block.astype(F32)
        sums = jnp.sum(sums, axis=1, keepdims=True)
        half = width // 2
        side = jnp.concatenate(
            [jnp.zeros((rank, half), F32), gram, jnp.zeros((rank, half - rank), F32)], axis=1
        )
        low = lax.broadcasted_iota(jnp.int32, (rank, width), 1) < half
        for c in range(total_ref.shape[1] // width):
            cols = slice(c * width, (c + 1) * width)
            block = (total_ref[:, cols] - mean_ref[:, cols] * sums) * scale_ref[:, cols]
            out_ref[2 * c] = jnp.where(low, block, side)
            out_ref[2 * c + 1] = jnp.where(low, pltpu.roll(block, half, 1), side)


def project_partial(genotype, sketch, mean, scale):
    words, snps = genotype.shape
    chunks, rank, width = sketch.shape
    steps = words // width
    whole = lambda g: (0, 0)
    shape = (2 * snps // width, rank, width)
    return pl.pallas_call(
        project_kernel,
        grid=(steps,),
        in_specs=[
            pl.BlockSpec((width, snps), lambda g: (g, 0)),
            pl.BlockSpec(sketch.shape, lambda g: (0, 0, 0)),
            pl.BlockSpec((1, snps), whole),
            pl.BlockSpec((1, snps), whole),
        ],
        out_specs=pl.BlockSpec(shape, lambda g: (0, 0, 0)),
        out_shape=jax.ShapeDtypeStruct(shape, F32),
        scratch_shapes=[pltpu.VMEM((rank, snps), F32)],
        name="project",
    )(genotype, sketch, mean, scale)


def solve_kernel(parts_ref, out_ref):
    sources, rank, width = parts_ref.shape
    half = width // 2
    work = parts_ref[0]
    for source in range(1, sources):
        work = work + parts_ref[source]
    row = lax.broadcasted_iota(jnp.int32, (rank, width), 0)
    scales = jnp.zeros((rank, 1), F32)
    for k in range(rank):
        pivot_row = work[k : k + 1, :]
        column = work[:, half + k : half + k + 1]
        pivot = work[k : k + 1, half + k : half + k + 1]
        scales = jnp.where(row[:, 0:1] == k, lax.rsqrt(pivot), scales)
        factor = jnp.where(row[:, 0:1] > k, column / pivot, 0.0)
        work = work - factor * pivot_row
    chunk = (work * scales).astype(BF16)
    for target in range(out_ref.shape[0]):
        out_ref[target] = chunk


def solve(parts):
    return pl.pallas_call(
        solve_kernel, out_shape=jax.ShapeDtypeStruct(parts.shape, BF16), name="solve"
    )(parts)


def finish_kernel(parts_ref, out_ref):
    chunks, rank, width = parts_ref.shape
    half = width // 2
    low = lax.broadcasted_iota(jnp.int32, (rank, width), 1) < half
    for c in range(chunks // 2):
        first = parts_ref[2 * c].astype(F32)
        second = pltpu.roll(parts_ref[2 * c + 1].astype(F32), half, 1)
        out_ref[:, c * width : (c + 1) * width] = jnp.where(low, first, second)


def finish(parts):
    chunks, rank, width = parts.shape
    return pl.pallas_call(
        finish_kernel,
        out_shape=jax.ShapeDtypeStruct((rank, chunks * width // 2), F32),
        name="finish",
    )(parts)


def exchange(chunks, axis):
    return lax.all_to_all(chunks, axis, 0, 0, tiled=True)


def on_device(genotype, probe, allele_mean, allele_scale):
    mean, scale = allele_mean[None, :], allele_scale[None, :]
    parts = exchange(sketch_partial(genotype, probe, mean, scale), "snp")
    sketch = exchange(sum_and_copy(parts), "snp")
    parts = exchange(project_partial(genotype, sketch, mean, scale), "ind")
    return finish(exchange(solve(parts), "ind"))


def solution(mesh):
    in_specs = (P("ind", "snp"), P(None, "snp"), P("snp"), P("snp"))
    return jax.shard_map(
        on_device, mesh=mesh, in_specs=in_specs, out_specs=P(None, "snp"), check_vma=False
    )
```

```python
import functools

import jax
import jax.numpy as jnp
from jax import lax
from jax.experimental import pallas as pl
from jax.experimental.pallas import tpu as pltpu
from jax.sharding import PartitionSpec as P

F32, BF16 = jnp.float32, jnp.bfloat16
NT = (((1,), (1,)), ((), ()))
LANES = 128
HALF = 64
HBM = pl.BlockSpec(memory_space=pltpu.HBM)
VMEM = pl.BlockSpec(memory_space=pltpu.VMEM)


def params(mib):
    return pltpu.CompilerParams(vmem_limit_bytes=mib << 20)


def sketch_kernel(
    words_hbm, probe_hbm, mean_hbm, scale_hbm, out_ref, digits_ref, mean_ref, scale_ref,
    words, probe_ref, small_sems, big_sems,
):
    rank = probe_ref.shape[0]
    rows = words.shape[0] // big_sems.shape[0]
    small = [
        pltpu.make_async_copy(source, target, small_sems.at[i])
        for i, (source, target) in enumerate(
            ((probe_hbm, probe_ref), (scale_hbm, scale_ref), (mean_hbm, mean_ref))
        )
    ]
    big = [
        pltpu.make_async_copy(
            words_hbm.at[pl.ds(g * rows, rows)], words.at[pl.ds(g * rows, rows)], big_sems.at[g]
        )
        for g in range(big_sems.shape[0])
    ]
    for copy in small + big:
        copy.start()
    for copy in small:
        copy.wait()
    weight = probe_ref[...].astype(F32) * scale_ref[...]
    high = weight.astype(BF16)
    both_parts = jnp.concatenate([high.astype(F32), weight - high.astype(F32)], axis=0).astype(BF16)
    shift = jnp.sum(weight * mean_ref[...], axis=1, keepdims=True)
    for g, copy in enumerate(big):
        copy.wait()
        packed = words[g * rows : (g + 1) * rows, :]
        for p in range(4):
            digits = jnp.bitwise_and(packed, 3 << (2 * p)).astype(F32).astype(BF16)
            first = (4 * g + p) * rows
            digits_ref[first : first + rows, :] = digits
            both = lax.dot_general(both_parts, digits, NT, preferred_element_type=F32)
            total = (both[0:rank, :] + both[rank : 2 * rank, :]) * (0.25**p) - shift
            for q in range(rows // LANES):
                chunk = total[:, q * LANES : (q + 1) * LANES]
                out_ref[first // LANES + q] = chunk.astype(BF16)


def sketch_partial(genotype, probe, mean, scale, pieces):
    words, snps = genotype.shape
    rank = probe.shape[0]
    operands = [
        pltpu.with_memory_space_constraint(x, pltpu.HBM) for x in (genotype, probe, mean, scale)
    ]
    return pl.pallas_call(
        sketch_kernel,
        in_specs=[HBM] * 4,
        out_specs=[VMEM] * 4,
        out_shape=[
            pltpu.VMEM((4 * words // LANES, rank, LANES), BF16),
            pltpu.VMEM((4 * words, snps), BF16),
            pltpu.VMEM((1, snps), F32),
            pltpu.VMEM((1, snps), F32),
        ],
        scratch_shapes=[
            pltpu.VMEM((words, snps), jnp.int32),
            pltpu.VMEM((rank, snps), BF16),
            pltpu.SemaphoreType.DMA((3,)),
            pltpu.SemaphoreType.DMA((pieces,)),
        ],
        compiler_params=params(16),
        name="sketch",
    )(*operands)


def gather_kernel(parts_ref, out_ref):
    total = parts_ref[0].astype(F32)
    for source in range(1, parts_ref.shape[0]):
        total = total + parts_ref[source].astype(F32)
    chunk = total.astype(BF16)
    for target in range(out_ref.shape[0]):
        out_ref[target] = chunk


def sum_and_copy(parts):
    return pl.pallas_call(
        gather_kernel,
        in_specs=[VMEM],
        out_specs=VMEM,
        out_shape=jax.ShapeDtypeStruct(parts.shape, BF16),
        compiler_params=params(4),
        name="sumsnp",
    )(parts)


def project_kernel(pieces, digits_ref, sketch_ref, mean_ref, scale_ref, out_ref):
    chunks, rank, width = sketch_ref.shape
    blocks = [sketch_ref[b].astype(F32) for b in range(chunks)]
    plane = [(b * 4 * pieces // chunks) % 4 for b in range(chunks)]
    left = jnp.concatenate([blocks[b] * (0.25 ** plane[b]) for b in range(chunks)], axis=1)
    total = jnp.dot(left.astype(BF16), digits_ref[...], preferred_element_type=F32)
    sketch = jnp.concatenate(blocks, axis=1)
    sums = jnp.sum(sketch, axis=1, keepdims=True)
    sketch = sketch.astype(BF16)
    gram = lax.dot_general(sketch, sketch, NT, preferred_element_type=F32)
    high = gram.astype(BF16).astype(F32)
    side = jnp.concatenate(
        [jnp.zeros((rank, HALF), F32), high, gram - high, jnp.zeros((rank, HALF - 2 * rank), F32)],
        axis=1,
    )
    low = lax.broadcasted_iota(jnp.int32, (rank, width), 1) < HALF
    for c in range(total.shape[1] // width):
        cols = slice(c * width, (c + 1) * width)
        block = (total[:, cols] - mean_ref[:, cols] * sums) * scale_ref[:, cols]
        out_ref[2 * c] = jnp.where(low, block, side).astype(BF16)
        out_ref[2 * c + 1] = jnp.where(low, pltpu.roll(block, HALF, 1), side).astype(BF16)


def project_partial(digits, sketch, mean, scale, pieces):
    snps = digits.shape[1]
    _, rank, width = sketch.shape
    return pl.pallas_call(
        functools.partial(project_kernel, pieces),
        in_specs=[VMEM] * 4,
        out_specs=VMEM,
        out_shape=jax.ShapeDtypeStruct((snps // HALF, rank, width), BF16),
        compiler_params=params(8),
        name="project",
    )(digits, sketch, mean, scale)


def solve_kernel(parts_ref, out_ref):
    sources, rank, width = parts_ref.shape
    work = parts_ref[0].astype(F32)
    for source in range(1, sources):
        work = work + parts_ref[source].astype(F32)
    lane = lax.broadcasted_iota(jnp.int32, (rank, width), 1)
    low_part = pltpu.roll(work, width - rank, 1)
    work = jnp.where(lane < HALF, work, work + low_part)
    row = lax.broadcasted_iota(jnp.int32, (rank, 1), 0)
    scales = jnp.zeros((rank, 1), F32)
    for k in range(rank):
        pivot_row = work[k : k + 1, :]
        column = work[:, HALF + k : HALF + k + 1]
        pivot = work[k : k + 1, HALF + k : HALF + k + 1]
        scales = jnp.where(row == k, lax.rsqrt(pivot), scales)
        factor = jnp.where(row > k, column / pivot, 0.0)
        work = work - factor * pivot_row
    work = work * scales
    first = jnp.where(lane[0:8] < HALF, work[0:8], pltpu.roll(work[8:16], HALF, 1))
    chunk = jnp.concatenate([first, work[16:24]], axis=0).astype(BF16)
    for target in range(out_ref.shape[0]):
        out_ref[target] = chunk


def solve(parts):
    sources, _, width = parts.shape
    return pl.pallas_call(
        solve_kernel,
        in_specs=[VMEM],
        out_specs=VMEM,
        out_shape=jax.ShapeDtypeStruct((sources, 16, width), BF16),
        compiler_params=params(4),
        name="solve",
    )(parts)


def finish_kernel(parts_ref, out_ref):
    chunks, _, width = parts_ref.shape
    low = lax.broadcasted_iota(jnp.int32, (8, width), 1) < HALF
    for c in range(chunks // 2):
        cols = slice(c * width, (c + 1) * width)
        even, odd = parts_ref[2 * c].astype(F32), parts_ref[2 * c + 1].astype(F32)
        even_turned, odd_turned = pltpu.roll(even, HALF, 1), pltpu.roll(odd, HALF, 1)
        out_ref[0:8, cols] = jnp.where(low, even[0:8], odd_turned[0:8])
        out_ref[8:16, cols] = jnp.where(low, even_turned[0:8], odd[0:8])
        out_ref[16:24, cols] = jnp.where(low, even[8:16], odd_turned[8:16])


def finish(parts, rank):
    chunks, _, width = parts.shape
    return pl.pallas_call(
        finish_kernel,
        in_specs=[VMEM],
        out_specs=VMEM,
        out_shape=jax.ShapeDtypeStruct((rank, chunks * width // 2), F32),
        compiler_params=params(4),
        name="finish",
    )(parts)


def exchange(chunks, axis):
    return lax.all_to_all(chunks, axis, 0, 0, tiled=True)


def on_device(genotype, probe, allele_mean, allele_scale):
    mean, scale = allele_mean[None, :], allele_scale[None, :]
    pieces = max(1, genotype.shape[0] // 256)
    parts, digits, mean, scale = sketch_partial(genotype, probe, mean, scale, pieces)
    sketch = exchange(sum_and_copy(exchange(parts, "snp")), "snp")
    parts = exchange(project_partial(digits, sketch, mean, scale, pieces), "ind")
    return finish(exchange(solve(parts), "ind"), probe.shape[0])


def solution(mesh):
    in_specs = (P("ind", "snp"), P(None, "snp"), P("snp"), P("snp"))
    return jax.shard_map(
        on_device, mesh=mesh, in_specs=in_specs, out_specs=P(None, "snp"), check_vma=False
    )
```

```python
import functools

import jax
import jax.numpy as jnp
from jax import lax
from jax.experimental import pallas as pl
from jax.experimental.pallas import tpu as pltpu
from jax.sharding import PartitionSpec as P

F32, BF16, F8 = jnp.float32, jnp.bfloat16, jnp.float8_e4m3fn
NT = (((1,), (1,)), ((), ()))
LANES = 128
HALF = 64
HBM = pl.BlockSpec(memory_space=pltpu.HBM)
VMEM = pl.BlockSpec(memory_space=pltpu.VMEM)


def params(mib):
    return pltpu.CompilerParams(vmem_limit_bytes=mib << 20)


def eighths(values, count):
    pieces = []
    for _ in range(count):
        piece = values.astype(F8).astype(F32)
        pieces.append(piece)
        values = (values - piece) * 16.0
    return jnp.concatenate(pieces, axis=0).astype(F8)


def sketch_kernel(
    words_hbm, probe_hbm, mean_hbm, scale_hbm, out_ref, digits_ref, mean_ref, scale_ref,
    words, probe_ref, small_sems, big_sems,
):
    rank = probe_ref.shape[0]
    rows = words.shape[0] // big_sems.shape[0]
    small = [
        pltpu.make_async_copy(source, target, small_sems.at[i])
        for i, (source, target) in enumerate(
            ((probe_hbm, probe_ref), (scale_hbm, scale_ref), (mean_hbm, mean_ref))
        )
    ]
    big = [
        pltpu.make_async_copy(
            words_hbm.at[pl.ds(g * rows, rows)], words.at[pl.ds(g * rows, rows)], big_sems.at[g]
        )
        for g in range(big_sems.shape[0])
    ]
    for copy in small + big:
        copy.start()
    for copy in small:
        copy.wait()
    weight = probe_ref[...].astype(F32) * scale_ref[...]
    pieces = eighths(weight * 4096.0, 3)
    shift = jnp.sum(weight * mean_ref[...], axis=1, keepdims=True)
    for g, copy in enumerate(big):
        copy.wait()
        packed = words[g * rows : (g + 1) * rows, :]
        for p in range(4):
            digits = jnp.bitwise_and(packed, 3 << (2 * p)).astype(F32).astype(BF16)
            first = (4 * g + p) * rows
            for c in range(digits_ref.shape[0]):
                digits_ref[c, first : first + rows, :] = digits[:, c * LANES : (c + 1) * LANES]
            parts = lax.dot_general(pieces, digits.astype(F8), NT, preferred_element_type=F32)
            parts = parts * (0.25**p / 4096.0)
            total = parts[2 * rank : 3 * rank, :] * 2.0**-8 + parts[rank : 2 * rank, :] * 2.0**-4
            total = total + parts[0:rank, :] - shift
            for q in range(rows // LANES):
                chunk = total[:, q * LANES : (q + 1) * LANES]
                out_ref[first // LANES + q] = chunk.astype(BF16)


def sketch_partial(genotype, probe, mean, scale, pieces):
    words, snps = genotype.shape
    rank = probe.shape[0]
    operands = [
        pltpu.with_memory_space_constraint(x, pltpu.HBM) for x in (genotype, probe, mean, scale)
    ]
    return pl.pallas_call(
        sketch_kernel,
        in_specs=[HBM] * 4,
        out_specs=[VMEM] * 4,
        out_shape=[
            pltpu.VMEM((4 * words // LANES, rank, LANES), BF16),
            pltpu.VMEM((snps // LANES, 4 * words, LANES), BF16),
            pltpu.VMEM((1, snps), F32),
            pltpu.VMEM((1, snps), F32),
        ],
        scratch_shapes=[
            pltpu.VMEM((words, snps), jnp.int32),
            pltpu.VMEM((rank, snps), BF16),
            pltpu.SemaphoreType.DMA((3,)),
            pltpu.SemaphoreType.DMA((pieces,)),
        ],
        compiler_params=params(16),
        name="sketch",
    )(*operands)


def chip_kernel(parts_ref, out_ref):
    half = out_ref.shape[1]
    first = lax.rem(lax.axis_index("snp"), 2) * half
    for q in range(half):
        ours = parts_ref[first + q].astype(F32) + parts_ref[2 * half + first + q].astype(F32)
        chunk = ours.astype(BF16)
        for target in range(out_ref.shape[0]):
            out_ref[target, q] = chunk


def sum_on_chip(parts, chips):
    chunks, rank, width = parts.shape
    return pl.pallas_call(
        chip_kernel,
        in_specs=[VMEM],
        out_specs=VMEM,
        out_shape=pltpu.VMEM((chips, chunks // 4, rank, width), BF16),
        compiler_params=params(4),
        name="sumchip",
    )(parts)


def gather_kernel(parts_ref, out_ref):
    for q in range(out_ref.shape[0]):
        total = parts_ref[0, q].astype(F32)
        for source in range(1, parts_ref.shape[0]):
            total = total + parts_ref[source, q].astype(F32)
        out_ref[q] = total.astype(BF16)


def sum_over_chips(parts):
    return pl.pallas_call(
        gather_kernel,
        in_specs=[VMEM],
        out_specs=VMEM,
        out_shape=pltpu.VMEM(parts.shape[1:], BF16),
        compiler_params=params(4),
        name="sumsnp",
    )(parts)


def sum_over_snps(parts, size):
    pairs = [[i, i + 1] for i in range(0, size, 2)]
    rings = [list(range(core, size, 2)) for core in range(2)]
    both = lax.all_gather(parts, "snp", axis_index_groups=pairs, tiled=True)
    parts = sum_on_chip(both, size // 2)
    parts = lax.all_to_all(parts, "snp", 0, 0, axis_index_groups=rings, tiled=True)
    return lax.all_gather(sum_over_chips(parts), "snp", axis_index_groups=pairs, tiled=True)


def project_kernel(pieces, digits_ref, sketch_ref, mean_ref, scale_ref, out_ref):
    chunks, rank, width = sketch_ref.shape
    blocks = [sketch_ref[b].astype(F32) for b in range(chunks)]
    plane = [(b * 4 * pieces // chunks) % 4 for b in range(chunks)]
    left = jnp.concatenate([blocks[b] * (0.25 ** plane[b]) for b in range(chunks)], axis=1)
    left = left.astype(BF16)
    sketch = jnp.concatenate(blocks, axis=1)
    sums = jnp.sum(sketch, axis=1, keepdims=True)
    sketch = sketch.astype(BF16)
    gram = lax.dot_general(sketch, sketch, NT, preferred_element_type=F32)
    high = gram.astype(BF16).astype(F32)
    side = jnp.concatenate(
        [jnp.zeros((rank, HALF), F32), high, gram - high, jnp.zeros((rank, HALF - 2 * rank), F32)],
        axis=1,
    )
    low = lax.broadcasted_iota(jnp.int32, (rank, width), 1) < HALF
    for c in range(digits_ref.shape[0]):
        cols = slice(c * width, (c + 1) * width)
        total = jnp.dot(left, digits_ref[c], preferred_element_type=F32)
        block = (total - mean_ref[:, cols] * sums) * scale_ref[:, cols]
        out_ref[2 * c] = jnp.where(low, block, side).astype(BF16)
        out_ref[2 * c + 1] = jnp.where(low, pltpu.roll(block, HALF, 1), side).astype(BF16)


def project_partial(digits, sketch, mean, scale, pieces):
    snps = digits.shape[0] * digits.shape[2]
    _, rank, width = sketch.shape
    return pl.pallas_call(
        functools.partial(project_kernel, pieces),
        in_specs=[VMEM] * 4,
        out_specs=VMEM,
        out_shape=jax.ShapeDtypeStruct((snps // HALF, rank, width), BF16),
        compiler_params=params(8),
        name="project",
    )(digits, sketch, mean, scale)


def eliminate(work, rank):
    tiles = range(rank // 8)
    rows = [work[8 * t : 8 * t + 8, :] for t in tiles]
    columns = [
        {
            t: jnp.broadcast_to(rows[t][:, HALF + j : HALF + j + 1], (8, LANES))
            for t in tiles
            if t >= j // 8
        }
        for j in range(rank)
    ]
    sublane = lax.broadcasted_iota(jnp.int32, (8, LANES), 0)
    scales = [jnp.zeros((8, LANES), F32) for _ in tiles]
    for k in range(rank):
        own, at = divmod(k, 8)
        pivot = jnp.broadcast_to(columns[k][own][at : at + 1, :], (8, LANES))
        scales[own] = jnp.where(sublane == at, lax.rsqrt(pivot), scales[own])
        inverse = 1.0 / pivot
        factors = {t: columns[k][t] * inverse for t in tiles if t >= own}
        factors[own] = jnp.where(sublane > at, factors[own], 0.0)
        for j in range(k + 1, rank):
            entry = columns[k][j // 8][j % 8 : j % 8 + 1, :]
            for t in tiles:
                if t >= j // 8:
                    columns[j][t] = columns[j][t] - factors[t] * entry
        pivot_row = rows[own][at : at + 1, :]
        for t in tiles:
            if t >= own:
                rows[t] = rows[t] - factors[t] * pivot_row
    return [rows[t] * scales[t] for t in tiles]


def solve_kernel(parts_ref, out_ref):
    sources, rank, width = parts_ref.shape
    work = parts_ref[0].astype(F32)
    for source in range(1, sources):
        work = work + parts_ref[source].astype(F32)
    lane = lax.broadcasted_iota(jnp.int32, (rank, width), 1)
    low_part = pltpu.roll(work, width - rank, 1)
    work = jnp.where(lane < HALF, work, work + low_part)
    done = eliminate(work, rank)
    first = jnp.where(lane[0:8] < HALF, done[0], pltpu.roll(done[1], HALF, 1))
    chunk = jnp.concatenate([first, done[2]], axis=0).astype(BF16)
    for target in range(out_ref.shape[0]):
        out_ref[target] = chunk


def solve(parts):
    sources, _, width = parts.shape
    return pl.pallas_call(
        solve_kernel,
        in_specs=[VMEM],
        out_specs=VMEM,
        out_shape=jax.ShapeDtypeStruct((sources, 16, width), BF16),
        compiler_params=params(4),
        name="solve",
    )(parts)


def finish_kernel(parts_ref, out_ref):
    chunks, _, width = parts_ref.shape
    low = lax.broadcasted_iota(jnp.int32, (8, width), 1) < HALF
    for c in range(chunks // 2):
        cols = slice(c * width, (c + 1) * width)
        even, odd = parts_ref[2 * c].astype(F32), parts_ref[2 * c + 1].astype(F32)
        even_turned, odd_turned = pltpu.roll(even, HALF, 1), pltpu.roll(odd, HALF, 1)
        out_ref[0:8, cols] = jnp.where(low, even[0:8], odd_turned[0:8])
        out_ref[8:16, cols] = jnp.where(low, even_turned[0:8], odd[0:8])
        out_ref[16:24, cols] = jnp.where(low, even[8:16], odd_turned[8:16])


def finish(parts, rank):
    chunks, _, width = parts.shape
    return pl.pallas_call(
        finish_kernel,
        in_specs=[VMEM],
        out_specs=VMEM,
        out_shape=jax.ShapeDtypeStruct((rank, chunks * width // 2), F32),
        compiler_params=params(4),
        name="finish",
    )(parts)


def exchange(chunks, axis):
    return lax.all_to_all(chunks, axis, 0, 0, tiled=True)


def on_device(genotype, probe, allele_mean, allele_scale):
    mean, scale = allele_mean[None, :], allele_scale[None, :]
    pieces = max(1, genotype.shape[0] // 256)
    parts, digits, mean, scale = sketch_partial(genotype, probe, mean, scale, pieces)
    sketch = sum_over_snps(parts, lax.axis_size("snp"))
    parts = exchange(project_partial(digits, sketch, mean, scale, pieces), "ind")
    return finish(exchange(solve(parts), "ind"), probe.shape[0])


def solution(mesh):
    in_specs = (P("ind", "snp"), P(None, "snp"), P("snp"), P("snp"))
    return jax.shard_map(
        on_device, mesh=mesh, in_specs=in_specs, out_specs=P(None, "snp"), check_vma=False
    )
```

```python
import functools

import jax
import jax.numpy as jnp
from jax import lax
from jax.experimental import pallas as pl
from jax.experimental.pallas import tpu as pltpu
from jax.sharding import PartitionSpec as P

F32, BF16, F8 = jnp.float32, jnp.bfloat16, jnp.float8_e4m3fn
NT = (((1,), (1,)), ((), ()))
LANES = 128
HALF = 64
HBM = pl.BlockSpec(memory_space=pltpu.HBM)
VMEM = pl.BlockSpec(memory_space=pltpu.VMEM)


def params(mib):
    return pltpu.CompilerParams(vmem_limit_bytes=mib << 20)


def eighths(values, count):
    pieces = []
    for _ in range(count):
        piece = values.astype(F8).astype(F32)
        pieces.append(piece)
        values = (values - piece) * 16.0
    return jnp.concatenate(pieces, axis=0).astype(F8)


def sketch_kernel(
    words_hbm, probe_hbm, mean_hbm, scale_hbm, out_ref, digits_ref, mean_ref, scale_ref,
    words, probe_ref, small_sems, big_sems,
):
    rank = probe_ref.shape[0]
    rows = words.shape[0] // big_sems.shape[0]
    small = [
        pltpu.make_async_copy(source, target, small_sems.at[i])
        for i, (source, target) in enumerate(
            ((probe_hbm, probe_ref), (scale_hbm, scale_ref), (mean_hbm, mean_ref))
        )
    ]
    big = [
        pltpu.make_async_copy(
            words_hbm.at[pl.ds(g * rows, rows)], words.at[pl.ds(g * rows, rows)], big_sems.at[g]
        )
        for g in range(big_sems.shape[0])
    ]
    for copy in small + big:
        copy.start()
    for copy in small:
        copy.wait()
    weight = probe_ref[...].astype(F32) * scale_ref[...]
    pieces = eighths(weight * 4096.0, 3)
    shift = jnp.sum(weight * mean_ref[...], axis=1, keepdims=True)
    for g, copy in enumerate(big):
        copy.wait()
        packed = words[g * rows : (g + 1) * rows, :]
        for p in range(4):
            digits = jnp.bitwise_and(packed, 3 << (2 * p)).astype(F32).astype(BF16)
            first = (4 * g + p) * rows
            for c in range(digits_ref.shape[0]):
                digits_ref[c, first : first + rows, :] = digits[:, c * LANES : (c + 1) * LANES]
            parts = lax.dot_general(pieces, digits.astype(F8), NT, preferred_element_type=F32)
            parts = parts * (0.25**p / 4096.0)
            total = parts[2 * rank : 3 * rank, :] * 2.0**-8 + parts[rank : 2 * rank, :] * 2.0**-4
            total = total + parts[0:rank, :] - shift
            for q in range(rows // LANES):
                chunk = total[:, q * LANES : (q + 1) * LANES]
                out_ref[first // LANES + q] = chunk.astype(BF16)


def sketch_partial(genotype, probe, mean, scale, pieces):
    words, snps = genotype.shape
    rank = probe.shape[0]
    operands = [
        pltpu.with_memory_space_constraint(x, pltpu.HBM) for x in (genotype, probe, mean, scale)
    ]
    return pl.pallas_call(
        sketch_kernel,
        in_specs=[HBM] * 4,
        out_specs=[VMEM] * 4,
        out_shape=[
            pltpu.VMEM((4 * words // LANES, rank, LANES), BF16),
            pltpu.VMEM((snps // LANES, 4 * words, LANES), BF16),
            pltpu.VMEM((1, snps), F32),
            pltpu.VMEM((1, snps), F32),
        ],
        scratch_shapes=[
            pltpu.VMEM((words, snps), jnp.int32),
            pltpu.VMEM((rank, snps), BF16),
            pltpu.SemaphoreType.DMA((3,)),
            pltpu.SemaphoreType.DMA((pieces,)),
        ],
        compiler_params=params(16),
        name="sketch",
    )(*operands)


def chip_kernel(parts_ref, out_ref):
    half = out_ref.shape[1]
    first = lax.rem(lax.axis_index("snp"), 2) * half
    for q in range(half):
        ours = parts_ref[first + q].astype(F32) + parts_ref[2 * half + first + q].astype(F32)
        chunk = ours.astype(BF16)
        for target in range(out_ref.shape[0]):
            out_ref[target, q] = chunk


def sum_on_chip(parts, chips):
    chunks, rank, width = parts.shape
    return pl.pallas_call(
        chip_kernel,
        in_specs=[VMEM],
        out_specs=VMEM,
        out_shape=pltpu.VMEM((chips, chunks // 4, rank, width), BF16),
        compiler_params=params(4),
        name="sumchip",
    )(parts)


def gather_kernel(parts_ref, out_ref):
    for q in range(out_ref.shape[0]):
        total = parts_ref[0, q].astype(F32)
        for source in range(1, parts_ref.shape[0]):
            total = total + parts_ref[source, q].astype(F32)
        out_ref[q] = total.astype(BF16)


def sum_over_chips(parts):
    return pl.pallas_call(
        gather_kernel,
        in_specs=[VMEM],
        out_specs=VMEM,
        out_shape=pltpu.VMEM(parts.shape[1:], BF16),
        compiler_params=params(4),
        name="sumsnp",
    )(parts)


def sum_over_snps(parts, size):
    pairs = [[i, i + 1] for i in range(0, size, 2)]
    rings = [list(range(core, size, 2)) for core in range(2)]
    both = lax.all_gather(parts, "snp", axis_index_groups=pairs, tiled=True)
    parts = sum_on_chip(both, size // 2)
    parts = lax.all_to_all(parts, "snp", 0, 0, axis_index_groups=rings, tiled=True)
    return lax.all_gather(sum_over_chips(parts), "snp", axis_index_groups=pairs, tiled=True)


def power_below(top):
    return jnp.floor(jnp.log2(32000.0 / jnp.maximum(top, 1e-30)))


def blocks_of(rank):
    return [(j, t) for j in range(rank // 8) for t in range(j, rank // 8)]


def project_kernel(pieces, digits_ref, sketch_ref, mean_ref, scale_ref, out_ref, product_ref):
    chunks, rank, width = sketch_ref.shape
    blocks = [sketch_ref[b].astype(F32) for b in range(chunks)]
    plane = [(b * 4 * pieces // chunks) % 4 for b in range(chunks)]
    left = jnp.concatenate([blocks[b] * (0.25 ** plane[b]) for b in range(chunks)], axis=1)
    left = left.astype(BF16)
    sketch = jnp.concatenate(blocks, axis=1)
    sums = jnp.sum(sketch, axis=1, keepdims=True)
    sketch = sketch.astype(BF16)
    gram = lax.dot_general(sketch, sketch, NT, preferred_element_type=F32)
    top = jnp.zeros((rank, width), F32)
    for c in range(digits_ref.shape[0]):
        cols = slice(c * width, (c + 1) * width)
        total = jnp.dot(left, digits_ref[c], preferred_element_type=F32)
        block = (total - mean_ref[:, cols] * sums) * scale_ref[:, cols]
        product_ref[:, cols] = block
        top = jnp.maximum(top, jnp.abs(block))
    power = power_below(jnp.max(top, axis=1, keepdims=True))
    gram_power = power_below(jnp.max(jnp.max(jnp.abs(gram), axis=1, keepdims=True), axis=0, keepdims=True))
    gram = gram * jnp.exp2(gram_power)
    sides = [gram[8 * t : 8 * t + 8, 8 * j : 8 * j + 8] for j, t in blocks_of(rank)]
    sides += [power[0:8], power[8:16], power[16:24], jnp.broadcast_to(gram_power, (8, 1))]
    used = 8 * len(blocks_of(rank)) + 4
    side = jnp.concatenate(
        [jnp.zeros((8, HALF), F32)] + sides + [jnp.zeros((8, HALF - used), F32)], axis=1
    )
    low = lax.broadcasted_iota(jnp.int32, (8, width), 1) < HALF
    factor = jnp.broadcast_to(jnp.exp2(power), (rank, width))
    for c in range(digits_ref.shape[0]):
        block = product_ref[:, c * width : (c + 1) * width] * factor
        tiles = [block[0:8], block[8:16], block[16:24]]
        turned = [pltpu.roll(tile, HALF, 1) for tile in tiles]
        even = [jnp.where(low, tiles[0], turned[1]), jnp.where(low, tiles[2], side)]
        odd = [jnp.where(low, turned[0], tiles[1]), jnp.where(low, turned[2], side)]
        for i, pair in enumerate((even, odd)):
            whole = jnp.round(jnp.concatenate(pair, axis=0)).astype(jnp.int32)
            out_ref[2 * c + i] = whole.astype(jnp.int16)


def project_partial(digits, sketch, mean, scale, pieces):
    snps = digits.shape[0] * digits.shape[2]
    _, rank, width = sketch.shape
    return pl.pallas_call(
        functools.partial(project_kernel, pieces),
        in_specs=[VMEM] * 4,
        out_specs=VMEM,
        out_shape=pltpu.VMEM((snps // HALF, 16, width), jnp.int16),
        scratch_shapes=[pltpu.VMEM((rank, snps), F32)],
        compiler_params=params(8),
        name="project",
    )(digits, sketch, mean, scale)


def eliminate(rows, columns):
    tiles = range(len(rows))
    rows = list(rows)
    sublane = lax.broadcasted_iota(jnp.int32, (8, LANES), 0)
    scales = [jnp.zeros((8, LANES), F32) for _ in tiles]
    for k in range(len(columns)):
        own, at = divmod(k, 8)
        pivot = jnp.broadcast_to(columns[k][own][at : at + 1, :], (8, LANES))
        scales[own] = jnp.where(sublane == at, lax.rsqrt(pivot), scales[own])
        inverse = 1.0 / pivot
        factors = {t: columns[k][t] * inverse for t in tiles if t >= own}
        factors[own] = jnp.where(sublane > at, factors[own], 0.0)
        for j in range(k + 1, len(columns)):
            entry = columns[k][j // 8][j % 8 : j % 8 + 1, :]
            for t in tiles:
                if t >= j // 8:
                    columns[j][t] = columns[j][t] - factors[t] * entry
        pivot_row = rows[own][at : at + 1, :]
        for t in tiles:
            if t >= own:
                rows[t] = rows[t] - factors[t] * pivot_row
    return [rows[t] * scales[t] for t in tiles]


def lane_of(tile, lane):
    return jnp.broadcast_to(tile[:, lane : lane + 1], tile.shape)


def solve_kernel(rank, parts_ref, out_ref):
    low = lax.broadcasted_iota(jnp.int32, (8, LANES), 1) < HALF
    order = blocks_of(rank)
    first_power = HALF + 8 * len(order)
    upper = jnp.zeros((8, LANES), F32)
    under = jnp.zeros((8, LANES), F32)
    for source in range(parts_ref.shape[0]):
        whole = parts_ref[source].astype(jnp.int32).astype(F32)
        inverse = jnp.exp2(-whole[8:16])
        steps = [lane_of(inverse, first_power + i) for i in range(4)]
        upper = upper + whole[0:8] * jnp.where(low, steps[0], steps[1])
        under = under + whole[8:16] * jnp.where(low, steps[2], steps[3])
    columns = [
        {t: lane_of(under, HALF + 8 * order.index((j // 8, t)) + j % 8) for t in range(j // 8, rank // 8)}
        for j in range(rank)
    ]
    done = eliminate([upper, pltpu.roll(upper, HALF, 1), under], columns)
    first = jnp.where(low, done[0], pltpu.roll(done[1], HALF, 1))
    chunk = jnp.concatenate([first, done[2]], axis=0).astype(BF16)
    for target in range(out_ref.shape[0]):
        out_ref[target] = chunk


def solve(parts, rank):
    return pl.pallas_call(
        functools.partial(solve_kernel, rank),
        in_specs=[VMEM],
        out_specs=VMEM,
        out_shape=jax.ShapeDtypeStruct(parts.shape, BF16),
        compiler_params=params(4),
        name="solve",
    )(parts)


def finish_kernel(parts_ref, out_ref):
    chunks, _, width = parts_ref.shape
    low = lax.broadcasted_iota(jnp.int32, (8, width), 1) < HALF
    for c in range(chunks // 2):
        cols = slice(c * width, (c + 1) * width)
        even, odd = parts_ref[2 * c].astype(F32), parts_ref[2 * c + 1].astype(F32)
        even_turned, odd_turned = pltpu.roll(even, HALF, 1), pltpu.roll(odd, HALF, 1)
        out_ref[0:8, cols] = jnp.where(low, even[0:8], odd_turned[0:8])
        out_ref[8:16, cols] = jnp.where(low, even_turned[0:8], odd[0:8])
        out_ref[16:24, cols] = jnp.where(low, even[8:16], odd_turned[8:16])


def finish(parts, rank):
    chunks, _, width = parts.shape
    return pl.pallas_call(
        finish_kernel,
        in_specs=[VMEM],
        out_specs=VMEM,
        out_shape=jax.ShapeDtypeStruct((rank, chunks * width // 2), F32),
        compiler_params=params(4),
        name="finish",
    )(parts)


def exchange(chunks, axis):
    return lax.all_to_all(chunks, axis, 0, 0, tiled=True)


def on_device(genotype, probe, allele_mean, allele_scale):
    mean, scale = allele_mean[None, :], allele_scale[None, :]
    pieces = max(1, genotype.shape[0] // 256)
    parts, digits, mean, scale = sketch_partial(genotype, probe, mean, scale, pieces)
    sketch = sum_over_snps(parts, lax.axis_size("snp"))
    parts = exchange(project_partial(digits, sketch, mean, scale, pieces), "ind")
    return finish(exchange(solve(parts, probe.shape[0]), "ind"), probe.shape[0])


def solution(mesh):
    in_specs = (P("ind", "snp"), P(None, "snp"), P("snp"), P("snp"))
    return jax.shard_map(
        on_device, mesh=mesh, in_specs=in_specs, out_specs=P(None, "snp"), check_vma=False
    )
```

```python
import functools

import jax
import jax.numpy as jnp
from jax import lax
from jax.experimental import pallas as pl
from jax.experimental.pallas import tpu as pltpu
from jax.sharding import PartitionSpec as P

F32, BF16 = jnp.float32, jnp.bfloat16
NT = (((1,), (1,)), ((), ()))
LANES = 128
HALF = 64
HBM = pl.BlockSpec(memory_space=pltpu.HBM)
VMEM = pl.BlockSpec(memory_space=pltpu.VMEM)


def params(mib):
    return pltpu.CompilerParams(vmem_limit_bytes=mib << 20)


def sketch_kernel(
    words_hbm, probe_hbm, mean_hbm, scale_hbm, out_ref, digits_ref, mean_ref, scale_ref,
    words, probe_ref, small_sems, big_sems,
):
    rank = probe_ref.shape[0]
    rows = words.shape[0] // big_sems.shape[0]
    small = [
        pltpu.make_async_copy(source, target, small_sems.at[i])
        for i, (source, target) in enumerate(
            ((probe_hbm, probe_ref), (scale_hbm, scale_ref), (mean_hbm, mean_ref))
        )
    ]
    big = [
        pltpu.make_async_copy(
            words_hbm.at[pl.ds(g * rows, rows)], words.at[pl.ds(g * rows, rows)], big_sems.at[g]
        )
        for g in range(big_sems.shape[0])
    ]
    for copy in small + big:
        copy.start()
    for copy in small:
        copy.wait()
    weight = probe_ref[...].astype(F32) * scale_ref[...]
    high = weight.astype(BF16)
    both_parts = jnp.concatenate([high.astype(F32), weight - high.astype(F32)], axis=0).astype(BF16)
    shift = jnp.sum(weight * mean_ref[...], axis=1, keepdims=True)
    for g, copy in enumerate(big):
        copy.wait()
        packed = words[g * rows : (g + 1) * rows, :]
        for p in range(4):
            digits = jnp.bitwise_and(packed, 3 << (2 * p)).astype(F32).astype(BF16)
            first = (4 * g + p) * rows
            for c in range(digits_ref.shape[0]):
                digits_ref[c, first : first + rows, :] = digits[:, c * LANES : (c + 1) * LANES]
            both = lax.dot_general(both_parts, digits, NT, preferred_element_type=F32)
            total = (both[0:rank, :] + both[rank : 2 * rank, :]) * (0.25**p) - shift
            for q in range(rows // LANES):
                chunk = total[:, q * LANES : (q + 1) * LANES]
                out_ref[first // LANES + q] = chunk.astype(BF16)


def sketch_partial(genotype, probe, mean, scale, pieces):
    words, snps = genotype.shape
    rank = probe.shape[0]
    operands = [
        pltpu.with_memory_space_constraint(x, pltpu.HBM) for x in (genotype, probe, mean, scale)
    ]
    return pl.pallas_call(
        sketch_kernel,
        in_specs=[HBM] * 4,
        out_specs=[VMEM] * 4,
        out_shape=[
            pltpu.VMEM((4 * words // LANES, rank, LANES), BF16),
            pltpu.VMEM((snps // LANES, 4 * words, LANES), BF16),
            pltpu.VMEM((1, snps), F32),
            pltpu.VMEM((1, snps), F32),
        ],
        scratch_shapes=[
            pltpu.VMEM((words, snps), jnp.int32),
            pltpu.VMEM((rank, snps), BF16),
            pltpu.SemaphoreType.DMA((3,)),
            pltpu.SemaphoreType.DMA((pieces,)),
        ],
        compiler_params=params(16),
        name="sketch",
    )(*operands)


def chip_kernel(parts_ref, out_ref):
    half = out_ref.shape[1]
    first = lax.rem(lax.axis_index("snp"), 2) * half
    for q in range(half):
        ours = parts_ref[first + q].astype(F32) + parts_ref[2 * half + first + q].astype(F32)
        chunk = ours.astype(BF16)
        for target in range(out_ref.shape[0]):
            out_ref[target, q] = chunk


def sum_on_chip(parts, chips):
    chunks, rank, width = parts.shape
    return pl.pallas_call(
        chip_kernel,
        in_specs=[VMEM],
        out_specs=VMEM,
        out_shape=pltpu.VMEM((chips, chunks // 4, rank, width), BF16),
        compiler_params=params(4),
        name="sumchip",
    )(parts)


def gather_kernel(parts_ref, out_ref):
    for q in range(out_ref.shape[0]):
        total = parts_ref[0, q].astype(F32)
        for source in range(1, parts_ref.shape[0]):
            total = total + parts_ref[source, q].astype(F32)
        out_ref[q] = total.astype(BF16)


def sum_over_chips(parts):
    return pl.pallas_call(
        gather_kernel,
        in_specs=[VMEM],
        out_specs=VMEM,
        out_shape=pltpu.VMEM(parts.shape[1:], BF16),
        compiler_params=params(4),
        name="sumsnp",
    )(parts)


def sum_over_snps(parts, size):
    pairs = [[i, i + 1] for i in range(0, size, 2)]
    rings = [list(range(core, size, 2)) for core in range(2)]
    both = lax.all_gather(parts, "snp", axis_index_groups=pairs, tiled=True)
    parts = sum_on_chip(both, size // 2)
    parts = lax.all_to_all(parts, "snp", 0, 0, axis_index_groups=rings, tiled=True)
    return lax.all_gather(sum_over_chips(parts), "snp", axis_index_groups=pairs, tiled=True)


def power_below(top):
    return jnp.floor(jnp.log2(32000.0 / jnp.maximum(top, 1e-30)))


def blocks_of(rank):
    return [(j, t) for j in range(rank // 8) for t in range(j, rank // 8)]


def project_kernel(pieces, digits_ref, sketch_ref, mean_ref, scale_ref, out_ref, product_ref):
    chunks, rank, width = sketch_ref.shape
    blocks = [sketch_ref[b].astype(F32) for b in range(chunks)]
    plane = [(b * 4 * pieces // chunks) % 4 for b in range(chunks)]
    left = jnp.concatenate([blocks[b] * (0.25 ** plane[b]) for b in range(chunks)], axis=1)
    left = left.astype(BF16)
    sketch = jnp.concatenate(blocks, axis=1)
    sums = jnp.sum(sketch, axis=1, keepdims=True)
    sketch = sketch.astype(BF16)
    gram = lax.dot_general(sketch, sketch, NT, preferred_element_type=F32)
    top = jnp.zeros((rank, width), F32)
    for c in range(digits_ref.shape[0]):
        cols = slice(c * width, (c + 1) * width)
        total = jnp.dot(left, digits_ref[c], preferred_element_type=F32)
        block = (total - mean_ref[:, cols] * sums) * scale_ref[:, cols]
        product_ref[:, cols] = block
        top = jnp.maximum(top, jnp.abs(block))
    power = power_below(jnp.max(top, axis=1, keepdims=True))
    gram_power = power_below(jnp.max(jnp.max(jnp.abs(gram), axis=1, keepdims=True), axis=0, keepdims=True))
    gram = gram * jnp.exp2(gram_power)
    sides = [gram[8 * t : 8 * t + 8, 8 * j : 8 * j + 8] for j, t in blocks_of(rank)]
    sides += [power[0:8], power[8:16], power[16:24], jnp.broadcast_to(gram_power, (8, 1))]
    used = 8 * len(blocks_of(rank)) + 4
    side = jnp.concatenate(
        [jnp.zeros((8, HALF), F32)] + sides + [jnp.zeros((8, HALF - used), F32)], axis=1
    )
    low = lax.broadcasted_iota(jnp.int32, (8, width), 1) < HALF
    factor = jnp.broadcast_to(jnp.exp2(power), (rank, width))
    for c in range(digits_ref.shape[0]):
        block = product_ref[:, c * width : (c + 1) * width] * factor
        tiles = [block[0:8], block[8:16], block[16:24]]
        turned = [pltpu.roll(tile, HALF, 1) for tile in tiles]
        even = [jnp.where(low, tiles[0], turned[1]), jnp.where(low, tiles[2], side)]
        odd = [jnp.where(low, turned[0], tiles[1]), jnp.where(low, turned[2], side)]
        for i, pair in enumerate((even, odd)):
            whole = jnp.round(jnp.concatenate(pair, axis=0)).astype(jnp.int32)
            out_ref[2 * c + i] = whole.astype(jnp.int16)


def project_partial(digits, sketch, mean, scale, pieces):
    snps = digits.shape[0] * digits.shape[2]
    _, rank, width = sketch.shape
    return pl.pallas_call(
        functools.partial(project_kernel, pieces),
        in_specs=[VMEM] * 4,
        out_specs=VMEM,
        out_shape=pltpu.VMEM((snps // HALF, 16, width), jnp.int16),
        scratch_shapes=[pltpu.VMEM((rank, snps), F32)],
        compiler_params=params(8),
        name="project",
    )(digits, sketch, mean, scale)


def eliminate(rows, columns):
    tiles = range(len(rows))
    rows = list(rows)
    sublane = lax.broadcasted_iota(jnp.int32, (8, LANES), 0)
    scales = [jnp.zeros((8, LANES), F32) for _ in tiles]
    for k in range(len(columns)):
        own, at = divmod(k, 8)
        pivot = jnp.broadcast_to(columns[k][own][at : at + 1, :], (8, LANES))
        scales[own] = jnp.where(sublane == at, lax.rsqrt(pivot), scales[own])
        inverse = 1.0 / pivot
        factors = {t: columns[k][t] * inverse for t in tiles if t >= own}
        factors[own] = jnp.where(sublane > at, factors[own], 0.0)
        for j in range(k + 1, len(columns)):
            entry = columns[k][j // 8][j % 8 : j % 8 + 1, :]
            for t in tiles:
                if t >= j // 8:
                    columns[j][t] = columns[j][t] - factors[t] * entry
        pivot_row = rows[own][at : at + 1, :]
        for t in tiles:
            if t >= own:
                rows[t] = rows[t] - factors[t] * pivot_row
    return [rows[t] * scales[t] for t in tiles]


def lane_of(tile, lane):
    return jnp.broadcast_to(tile[:, lane : lane + 1], tile.shape)


def solve_kernel(rank, parts_ref, out_ref):
    low = lax.broadcasted_iota(jnp.int32, (8, LANES), 1) < HALF
    order = blocks_of(rank)
    first_power = HALF + 8 * len(order)
    upper = jnp.zeros((8, LANES), F32)
    under = jnp.zeros((8, LANES), F32)
    for source in range(parts_ref.shape[0]):
        whole = parts_ref[source].astype(jnp.int32).astype(F32)
        inverse = jnp.exp2(-whole[8:16])
        steps = [lane_of(inverse, first_power + i) for i in range(4)]
        upper = upper + whole[0:8] * jnp.where(low, steps[0], steps[1])
        under = under + whole[8:16] * jnp.where(low, steps[2], steps[3])
    columns = [
        {t: lane_of(under, HALF + 8 * order.index((j // 8, t)) + j % 8) for t in range(j // 8, rank // 8)}
        for j in range(rank)
    ]
    done = eliminate([upper, pltpu.roll(upper, HALF, 1), under], columns)
    first = jnp.where(low, done[0], pltpu.roll(done[1], HALF, 1))
    chunk = jnp.concatenate([first, done[2]], axis=0).astype(BF16)
    for target in range(out_ref.shape[0]):
        out_ref[target] = chunk


def solve(parts, rank):
    return pl.pallas_call(
        functools.partial(solve_kernel, rank),
        in_specs=[VMEM],
        out_specs=VMEM,
        out_shape=jax.ShapeDtypeStruct(parts.shape, BF16),
        compiler_params=params(4),
        name="solve",
    )(parts)


def finish_kernel(parts_ref, out_ref):
    chunks, _, width = parts_ref.shape
    low = lax.broadcasted_iota(jnp.int32, (8, width), 1) < HALF
    for c in range(chunks // 2):
        cols = slice(c * width, (c + 1) * width)
        even, odd = parts_ref[2 * c].astype(F32), parts_ref[2 * c + 1].astype(F32)
        even_turned, odd_turned = pltpu.roll(even, HALF, 1), pltpu.roll(odd, HALF, 1)
        out_ref[0:8, cols] = jnp.where(low, even[0:8], odd_turned[0:8])
        out_ref[8:16, cols] = jnp.where(low, even_turned[0:8], odd[0:8])
        out_ref[16:24, cols] = jnp.where(low, even[8:16], odd_turned[8:16])


def finish(parts, rank):
    chunks, _, width = parts.shape
    return pl.pallas_call(
        finish_kernel,
        in_specs=[VMEM],
        out_specs=VMEM,
        out_shape=jax.ShapeDtypeStruct((rank, chunks * width // 2), F32),
        compiler_params=params(4),
        name="finish",
    )(parts)


def exchange(chunks, axis):
    return lax.all_to_all(chunks, axis, 0, 0, tiled=True)


def on_device(genotype, probe, allele_mean, allele_scale):
    mean, scale = allele_mean[None, :], allele_scale[None, :]
    pieces = max(1, genotype.shape[0] // 256)
    parts, digits, mean, scale = sketch_partial(genotype, probe, mean, scale, pieces)
    sketch = sum_over_snps(parts, lax.axis_size("snp"))
    parts = exchange(project_partial(digits, sketch, mean, scale, pieces), "ind")
    return finish(exchange(solve(parts, probe.shape[0]), "ind"), probe.shape[0])


def solution(mesh):
    in_specs = (P("ind", "snp"), P(None, "snp"), P("snp"), P("snp"))
    return jax.shard_map(
        on_device, mesh=mesh, in_specs=in_specs, out_specs=P(None, "snp"), check_vma=False
    )
```
